32 devices in a mesh: pencil: 4 (over x, core), bulk: 8 (over z, y).
Axes of the slice: x: 2, y: 2, z: 4, core: 2. Of those that a mesh axis runs over, the one named last changes fastest.
Arguments:
- density: float32 [8, 128, 384, 384], P(None, 'bulk', 'pencil'), may hold values from -400 to 400
- start_first: float32 [384, 128], replicated, may hold values from -6 to 6
- start_second: float32 [384, 128], replicated, may hold values from -6 to 6
Outputs:
- core_tensor: float32 [8, 128, 128, 128], P(None, 'bulk', 'pencil')
- factor_first: float32 [384, 128], replicated
- factor_second: float32 [384, 128], replicated
The draws below stay inside these ranges and needn't reach their ends.
All inputs are finite; a program needn't handle non-finite values.
Results may differ from the reference program's by a relative error of at most 0.0003.
Values sent between devices are 32-bit elements; how exact they have to be, the bound alone decides.
No kernel may reach another device: no remote copies, remote signals or barrier semaphores. Data moves between devices by JAX's collectives and lax.ppermute only.
A program may use at most 128 MiB of HBM per device.

```python
import math
import jax
import jax.numpy as jnp
from jax import lax

M1 = 384
M2 = 384
RANK = 128
SNAPS = 8
ITERS = 3
M3 = 128


def mixing_matrix(key, width, decades):
    decay = jnp.exp(-decades * math.log(10.0) * jnp.arange(width, dtype=jnp.float32) / width)
    entries = jax.random.normal(key, (width, width), jnp.float32) * decay[None, :]
    return entries / jnp.sqrt(jnp.sum(decay * decay))


def smooth_shapes(key, width):
    phases = jax.random.uniform(key, (3,), jnp.float32, 0.0, 2.0 * math.pi)
    waves = jnp.arange(1, 4, dtype=jnp.float32)
    cells = jnp.arange(width, dtype=jnp.float32) / width
    return jnp.cos(2.0 * math.pi * cells[:, None] * waves[None, :] + phases[None, :])


def draw_density(key, part):
    keys = jax.random.split(key, 8)
    shape = (SNAPS, M3, M2, M1)
    third = 1.0 + 0.7 * jnp.arange(M3, dtype=jnp.float32) / max(M3 - 1, 1)
    second = jnp.exp(jax.random.uniform(keys[1], (M2,), jnp.float32, 0.0, math.log(2.0)))
    first = jnp.exp(jax.random.uniform(keys[0], (M1,), jnp.float32, 0.0, math.log(4.0)))
    noise = jax.random.truncated_normal(keys[2], -6.0, 6.0, shape, jnp.float32)
    decades = 2.0
    mix_first = mixing_matrix(keys[3], M1, decades)
    mix_second = mixing_matrix(keys[4], M2, decades)
    mixed = jnp.dot(noise.reshape(-1, M1), mix_first.T).reshape(shape)
    mixed = jnp.einsum('skmi,jm->skji', mixed, mix_second)
    amps = jax.random.truncated_normal(keys[5], -3.0, 3.0, (SNAPS, M3, 3), jnp.float32)
    shape_first = smooth_shapes(keys[6], M1)
    shape_second = smooth_shapes(keys[7], M2)
    coherent = 0.5 * jnp.einsum('skc,jc,ic->skji', amps, shape_second, shape_first)
    value = (mixed + coherent) * first[None, None, None, :] * second[None, None, :, None] * third[None, :, None, None]
    value = jnp.clip(value, -400.0, 400.0)
    return value.astype(jnp.float32)


def bell_draw(own_key, shape, spread, bound, held_as=jnp.bfloat16):
    return jnp.clip(spread * jax.random.normal(own_key, shape, jnp.float32), -bound, bound).astype(held_as)


def setup_inputs(seed: int = 0) -> dict:
    key_of = jax.random.split(jax.random.key(seed), 4)
    return {
        "density": draw_density(jax.random.fold_in(key_of[3], 71), 0),
        "start_first": bell_draw(key_of[1], (M1, RANK), 1.0, 6.0, jnp.float32),
        "start_second": bell_draw(key_of[2], (M2, RANK), 1.0, 6.0, jnp.float32),
    }


HIGHEST_PREC = lax.Precision.HIGHEST

def orthonormal(columns):
    moment = jnp.dot(columns.T.astype(jnp.float32), columns.astype(jnp.float32), precision=HIGHEST_PREC, preferred_element_type=jnp.float32)
    factor_low = jnp.linalg.cholesky(moment)
    return jax.scipy.linalg.solve_triangular(factor_low, columns.T, lower=True).T

def subspace(gram, start_basis):
    basis_now = start_basis
    for number in range(ITERS):
        basis_now = orthonormal(jnp.dot(gram.astype(jnp.float32), basis_now.astype(jnp.float32), precision=HIGHEST_PREC, preferred_element_type=jnp.float32))
    return basis_now

def reference(density, start_first, start_second):
    unfolded = density.reshape(-1, M1)
    gram_first = jnp.dot(unfolded.T.astype(jnp.float32), unfolded.astype(jnp.float32), precision=HIGHEST_PREC, preferred_element_type=jnp.float32)
    factor_first = subspace(gram_first, start_first)
    projected = jnp.dot(unfolded.astype(jnp.float32), factor_first.astype(jnp.float32), precision=HIGHEST_PREC, preferred_element_type=jnp.float32)
    projected = projected.reshape(SNAPS, M3, M2, RANK)
    second_flat = jnp.swapaxes(projected, 2, 3).reshape(-1, M2)
    gram_second = jnp.dot(second_flat.T.astype(jnp.float32), second_flat.astype(jnp.float32), precision=HIGHEST_PREC, preferred_element_type=jnp.float32)
    factor_second = subspace(gram_second, start_second)
    core_tensor = jnp.dot(second_flat.astype(jnp.float32), factor_second.astype(jnp.float32), precision=HIGHEST_PREC, preferred_element_type=jnp.float32)
    core_tensor = core_tensor.reshape(SNAPS, M3, RANK, RANK)
    return (core_tensor, factor_first, factor_second)
```

```python
import functools

import jax
import jax.numpy as jnp
from jax import lax
from jax.experimental import pallas as pl
from jax.experimental.pallas import tpu as pltpu
from jax.sharding import PartitionSpec as P

ITERS = 3
LANES = 128
CHUNKS = 4
PERMUTES = 16


def split(x):
    high = x.astype(jnp.bfloat16)
    return high, (x - high.astype(jnp.float32)).astype(jnp.bfloat16)


def mul(a, b, over_a, over_b, precision=None):
    return lax.dot_general(
        a,
        b,
        (((over_a,), (over_b,)), ((), ())),
        precision=precision,
        preferred_element_type=jnp.float32,
    )


exact = functools.partial(mul, precision=lax.Precision.HIGHEST)


def upper_blocks(width):
    count = width // LANES
    return [(p, q) for p in range(count) for q in range(p, count)]


def store_packed(sums, squares, out_ref):
    width = sums.shape[0]
    cross = sums[:, width:]
    gram = sums[:, :width] + cross + cross.T
    row = lax.broadcasted_iota(jnp.int32, gram.shape, 0)
    col = lax.broadcasted_iota(jnp.int32, gram.shape, 1)
    gram = gram + jnp.where(row == col, squares, 0.0)
    for place, (p, q) in enumerate(upper_blocks(width)):
        out_ref[place * LANES : (place + 1) * LANES] = gram[
            p * LANES : (p + 1) * LANES, q * LANES : (q + 1) * LANES
        ]


def gram_rows_kernel(x_ref, out_ref, acc, acc_sq):
    step = pl.program_id(0)

    @pl.when(step == 0)
    def _():
        acc[...] = jnp.zeros_like(acc)
        acc_sq[...] = jnp.zeros_like(acc_sq)

    x = x_ref[...]
    high = x.astype(jnp.bfloat16)
    rest = x - high.astype(jnp.float32)
    acc[...] += mul(high, jnp.concatenate([high, rest.astype(jnp.bfloat16)], 1), 0, 0)
    acc_sq[...] += jnp.sum((rest * rest).reshape(-1, 8, x.shape[1]), 0)

    @pl.when(step == pl.num_programs(0) - 1)
    def _():
        store_packed(acc[...], jnp.sum(acc_sq[...], 0, keepdims=True), out_ref)


def packed_rows(width):
    return len(upper_blocks(width)) * LANES


def gram_rows(x):
    rows, width = x.shape
    tile = rows // 4
    return pl.pallas_call(
        gram_rows_kernel,
        grid=(rows // tile,),
        in_specs=[pl.BlockSpec((tile, width), lambda i: (i, 0))],
        out_specs=pl.BlockSpec((packed_rows(width), LANES), lambda i: (0, 0)),
        out_shape=jax.ShapeDtypeStruct((packed_rows(width), LANES), jnp.float32),
        scratch_shapes=[
            pltpu.VMEM((width, 2 * width), jnp.float32),
            pltpu.VMEM((8, width), jnp.float32),
        ],
        name="gram_rows",
    )(x)


def partner(x, axis, size, offset):
    return lax.ppermute(x, axis, [(i, i ^ offset) for i in range(size)])


def reduce_all(packed, me, mesh_sizes):
    n, groups = mesh_sizes
    rows = packed.shape[0] // n
    blocks = packed.reshape(n, rows, packed.shape[1])
    total = lax.dynamic_index_in_dim(blocks, me, 0, keepdims=False)
    arrived = [
        partner(lax.dynamic_index_in_dim(blocks, me ^ d, 0, keepdims=False), "pencil", n, d)
        for d in range(1, n)
    ]
    for piece in arrived:
        total = total + piece
    offset = 1
    while offset < groups:
        total = total + partner(total, "bulk", groups, offset)
        offset *= 2
    return [total] + [partner(total, "pencil", n, d) for d in range(1, n)]


def eliminate(w):
    n = w.shape[0]
    lane = lax.broadcasted_iota(jnp.int32, (8, n), 1)
    sub = lax.broadcasted_iota(jnp.int32, (8, n), 0)
    out = []
    for k in range(0, n, 8):
        panel = w[:8]
        cols = [jnp.broadcast_to(panel[:, k + j : k + j + 1], (8, n)) for j in range(8)]
        inside = (lane >= k) & (lane < k + 8)
        panel = jnp.where(inside, jnp.where(lane - k == sub, 1.0, 0.0), panel)
        inverse = jnp.zeros((8, n), jnp.float32)
        for j in range(8):
            pivot = 1.0 / jnp.broadcast_to(cols[j][j : j + 1], (8, n))
            inverse = jnp.where(sub == j, pivot, inverse)
            if j < 7:
                factor = jnp.where(sub > j, cols[j] * pivot, 0.0)
                for q in range(j + 1, 8):
                    cols[q] = cols[q] - factor * jnp.broadcast_to(cols[q][j : j + 1], (8, n))
                panel = panel - factor * jnp.broadcast_to(panel[j : j + 1], (8, n))
        out.append(jnp.where(lane < k + 8, panel * jnp.sqrt(inverse), 0.0))
        left = n - k - 8
        if left:
            update = exact(panel * inverse, panel, 0, 0)[k + 8 :]
            lane_left = lax.broadcasted_iota(jnp.int32, (left, n), 1)
            inside = (lane_left >= k) & (lane_left < k + 8)
            w = jnp.where(inside, 0.0, w[8:]) - update
    return jnp.concatenate(out, 0)


def subspace_kernel(n, me_ref, *refs):
    pieces, (start_ref, out_ref, packed, gram) = refs[:n], refs[n:]
    rows = pieces[0].shape[0]
    for d, piece in enumerate(pieces):
        at = pl.multiple_of((me_ref[0] ^ d) * rows, 8)
        packed[pl.ds(at, rows), :] = piece[...]
    for place, (p, q) in enumerate(upper_blocks(gram.shape[0])):
        block = packed[place * LANES : (place + 1) * LANES]
        gram[p * LANES : (p + 1) * LANES, q * LANES : (q + 1) * LANES] = block
        if p != q:
            gram[q * LANES : (q + 1) * LANES, p * LANES : (p + 1) * LANES] = block.T
    out_ref[...] = start_ref[...]

    def iteration(_, carry):
        grown = exact(gram[...], out_ref[...], 1, 0)
        out_ref[...] = exact(grown, eliminate(exact(grown, grown, 0, 0)), 1, 1)
        return carry

    lax.fori_loop(0, ITERS, iteration, 0)


def subspace(me, pieces, start):
    width = start.shape[0]
    vmem = pl.BlockSpec(memory_space=pltpu.VMEM)
    return pl.pallas_call(
        functools.partial(subspace_kernel, len(pieces)),
        in_specs=[pl.BlockSpec(memory_space=pltpu.SMEM)] + [vmem] * (len(pieces) + 1),
        out_specs=vmem,
        out_shape=jax.ShapeDtypeStruct(start.shape, jnp.float32),
        scratch_shapes=[
            pltpu.VMEM((packed_rows(width), LANES), jnp.float32),
            pltpu.VMEM((width, width), jnp.float32),
        ],
        name="subspace",
    )(me, *pieces, start)


def project_kernel(n, x_ref, basis_ref, *out_refs):
    items, cols, width = x_ref.shape
    high, low = split(x_ref[...].reshape(items * cols, width))
    rank = basis_ref.shape[1]
    basis = jnp.concatenate(split(basis_ref[...]), 1)
    sums = mul(high, basis, 1, 0)
    projected = sums[:, :rank] + sums[:, rank:] + mul(low, basis[:, :rank], 1, 0)
    share = rank // n
    lane = lax.broadcasted_iota(jnp.int32, (cols, rank), 1)
    for d, out_ref in enumerate(out_refs):
        piece = None
        for m in range(items):
            part = projected[m * cols : (m + 1) * cols]
            turn = (m - d) * share % rank
            if turn:
                part = pltpu.roll(part, turn, 1)
            piece = part if m == 0 else jnp.where(lane >= m * share, part, piece)
        out_ref[...] = piece


def project(x, basis, n, chunk, chunks):
    items, cols, width = x.shape
    rank = basis.shape[1]
    steps = items // n // chunks
    return pl.pallas_call(
        functools.partial(project_kernel, n),
        grid=(steps,),
        in_specs=[
            pl.BlockSpec((n, cols, width), lambda i: (chunk * steps + i, 0, 0)),
            pl.BlockSpec((width, rank), lambda i: (0, 0)),
        ],
        out_specs=[pl.BlockSpec((cols, rank), lambda i: (0, i))] * n,
        out_shape=[jax.ShapeDtypeStruct((cols, steps * rank), jnp.float32)] * n,
        cost_estimate=pl.CostEstimate(
            flops=6 * items // chunks * cols * width * rank,
            bytes_accessed=4 * items // chunks * cols * (width + rank),
            transcendentals=0,
        ),
        name="project",
    )(x, basis)


def stack(me_ref, pieces, high_ref, low_ref):
    cols = pieces[0].shape[0]
    for d, piece in enumerate(pieces):
        at = pl.multiple_of((me_ref[0] ^ d) * cols, 16)
        high, low = split(piece[...])
        high_ref[pl.ds(at, cols), :] = high
        low_ref[pl.ds(at, cols), :] = low


def gram_cols_kernel(n, me_ref, *refs):
    pieces, (before_ref, sums_ref, packed_ref, both) = refs[:n], refs[n:]
    width = both.shape[0] // 2

    @pl.when(pl.program_id(0) == 0)
    def _():
        sums_ref[...] = before_ref[...]

    stack(me_ref, pieces, both.at[:width], both.at[width:])
    sums_ref[:, : 2 * width] += mul(both[:width], both[...], 1, 1)
    low = both[width:].astype(jnp.float32)
    sums_ref[:, 2 * width :] += jnp.broadcast_to(
        jnp.sum(low * low, 1, keepdims=True), (width, LANES)
    )

    @pl.when(pl.program_id(0) == pl.num_programs(0) - 1)
    def _():
        squares = sums_ref[:, 2 * width :][:, :1]
        store_packed(sums_ref[:, : 2 * width], squares, packed_ref)


def gram_cols(me, pieces, before):
    n = len(pieces)
    cols, length = pieces[0].shape
    width = n * cols
    tile = length
    whole = pl.BlockSpec(before.shape, lambda i: (0, 0))
    return pl.pallas_call(
        functools.partial(gram_cols_kernel, n),
        grid=(length // tile,),
        in_specs=[pl.BlockSpec(memory_space=pltpu.SMEM)]
        + [pl.BlockSpec((cols, tile), lambda i: (0, i))] * n
        + [whole],
        out_specs=[whole, pl.BlockSpec((packed_rows(width), LANES), lambda i: (0, 0))],
        out_shape=[
            jax.ShapeDtypeStruct(before.shape, jnp.float32),
            jax.ShapeDtypeStruct((packed_rows(width), LANES), jnp.float32),
        ],
        scratch_shapes=[pltpu.VMEM((2 * width, tile), jnp.bfloat16)],
        cost_estimate=pl.CostEstimate(
            flops=4 * width * width * length,
            bytes_accessed=4 * width * length,
            transcendentals=0,
        ),
        name="gram_cols",
    )(me, *pieces, before)


def core_kernel(chunks, n, me_ref, *refs):
    pieces, (basis_ref, out_ref, high, low) = refs[: chunks * n], refs[chunks * n :]
    rank = basis_ref.shape[1]
    basis = jnp.concatenate(split(basis_ref[...]), 1)
    for chunk in range(chunks):

        @pl.when(pl.program_id(0) == chunk)
        def _():
            stack(me_ref, pieces[chunk * n : (chunk + 1) * n], high, low)

    sums = mul(high[...], basis, 0, 0)
    out_ref[...] = sums[:, :rank] + sums[:, rank:] + mul(low[...], basis[:, :rank], 0, 0)


def core(me, pieces, basis):
    chunks, n = len(pieces), len(pieces[0])
    cols, length = pieces[0][0].shape
    rank = basis.shape[1]
    tile = length
    steps = length // tile

    def held(chunk):
        return lambda c, i: (0, jnp.clip((c - chunk) * steps + i, 0, steps - 1))

    return pl.pallas_call(
        functools.partial(core_kernel, chunks, n),
        grid=(chunks, steps),
        in_specs=[pl.BlockSpec(memory_space=pltpu.SMEM)]
        + [pl.BlockSpec((cols, tile), held(c)) for c in range(chunks) for _ in range(n)]
        + [pl.BlockSpec(basis.shape, lambda c, i: (0, 0))],
        out_specs=pl.BlockSpec((tile, rank), lambda c, i: (c * steps + i, 0)),
        out_shape=jax.ShapeDtypeStruct((chunks * length, rank), jnp.float32),
        scratch_shapes=[pltpu.VMEM((n * cols, tile), jnp.bfloat16)] * 2,
        name="core",
    )(me, *[piece for group in pieces for piece in group], basis)


def per_device(n, groups, density, start_first, start_second):
    snap_count, cell_count, my_cols, mode_width = density.shape
    rank = start_first.shape[1]
    place = lax.axis_index("pencil")
    me = place.astype(jnp.int32).reshape(1)
    items = density.reshape(snap_count * cell_count, my_cols, mode_width)

    packed = gram_rows(density.reshape(-1, mode_width))
    factor_first = subspace(me, reduce_all(packed, place, (n, groups)), start_first)

    order = factor_first.reshape(mode_width, n, rank // n)
    order = jnp.concatenate([lax.dynamic_slice_in_dim(order, place ^ d, 1, 1) for d in range(n)], 1)
    basis = order.reshape(mode_width, rank)
    pieces = []
    for chunk in range(CHUNKS):
        own, *sent = project(items, basis, n, chunk, CHUNKS)
        pieces.append([own] + [partner(x, "pencil", n, d + 1) for d, x in enumerate(sent)])

    width = n * my_cols
    sums = jnp.zeros((width, 2 * width + LANES), jnp.float32)
    for group in pieces:
        sums, packed = gram_cols(me, group, sums)
    factor_second = subspace(me, reduce_all(packed, place, (n, groups)), start_second)

    core_tensor = core(me, pieces, factor_second)
    core_tensor = core_tensor.reshape(snap_count, cell_count, rank // n, factor_second.shape[1])
    return (core_tensor, factor_first, factor_second)


def solution(mesh):
    placed = (P(None, "bulk", "pencil", None), P(), P())
    return jax.shard_map(
        functools.partial(per_device, mesh.shape["pencil"], mesh.shape["bulk"]),
        mesh=mesh,
        in_specs=placed,
        out_specs=(P(None, "bulk", "pencil", None), P(), P()),
        check_vma=False,
    )
```

```python
import functools

import jax
import jax.numpy as jnp
from jax import lax
from jax.experimental import pallas as pl
from jax.experimental.pallas import tpu as pltpu
from jax.sharding import PartitionSpec as P

ITERS = 3
LANES = 128
SUPER = 64
GROUPS = 4
PERMUTES = 16

SCALAR = pl.BlockSpec(memory_space=pltpu.SMEM)


def split(x):
    high = x.astype(jnp.bfloat16)
    return high, (x - high.astype(jnp.float32)).astype(jnp.bfloat16)


def mul(a, b, over_a, over_b, precision=None):
    return lax.dot_general(
        a,
        b,
        (((over_a,), (over_b,)), ((), ())),
        precision=precision,
        preferred_element_type=jnp.float32,
    )


exact = functools.partial(mul, precision=lax.Precision.HIGHEST)


def upper_blocks(width):
    count = width // LANES
    return [(p, q) for p in range(count) for q in range(p, count)]


def packed_rows(width):
    return len(upper_blocks(width)) * LANES


def store_pieces(me_ref, gram, packed, out_refs):
    for place, (p, q) in enumerate(upper_blocks(gram.shape[0])):
        packed[place * LANES : (place + 1) * LANES] = gram[
            p * LANES : (p + 1) * LANES, q * LANES : (q + 1) * LANES
        ]
    for d, out_ref in enumerate(out_refs):
        rows = out_ref.shape[0]
        at = pl.multiple_of((me_ref[0] ^ d) * rows, 8)
        out_ref[...] = packed[pl.ds(at, rows), :]


def piece_outputs(n, width):
    shape = (packed_rows(width) // n, LANES)
    return (
        [pl.BlockSpec(shape, lambda i: (0, 0))] * n,
        [jax.ShapeDtypeStruct(shape, jnp.float32)] * n,
    )


def gram_rows_kernel(me_ref, x_ref, *refs):
    out_refs, (acc, acc_sq, packed) = refs[:-3], refs[-3:]
    step = pl.program_id(0)

    @pl.when(step == 0)
    def _():
        acc[...] = jnp.zeros_like(acc)
        acc_sq[...] = jnp.zeros_like(acc_sq)

    x = x_ref[...]
    high = x.astype(jnp.bfloat16)
    rest = x - high.astype(jnp.float32)
    acc[...] += mul(high, jnp.concatenate([high, rest.astype(jnp.bfloat16)], 1), 0, 0)
    acc_sq[...] += jnp.sum((rest * rest).reshape(-1, 8, x.shape[1]), 0)

    @pl.when(step == pl.num_programs(0) - 1)
    def _():
        width = x.shape[1]
        cross = acc[:, width:]
        gram = acc[:, :width] + cross + cross.T
        row = lax.broadcasted_iota(jnp.int32, gram.shape, 0)
        col = lax.broadcasted_iota(jnp.int32, gram.shape, 1)
        squares = jnp.sum(acc_sq[...], 0, keepdims=True)
        store_pieces(me_ref, gram + jnp.where(row == col, squares, 0.0), packed, out_refs)


def gram_rows(me, x, n):
    rows, width = x.shape
    tile = rows // 4
    specs, shapes = piece_outputs(n, width)
    return pl.pallas_call(
        gram_rows_kernel,
        grid=(rows // tile,),
        in_specs=[SCALAR, pl.BlockSpec((tile, width), lambda i: (i, 0))],
        out_specs=specs,
        out_shape=shapes,
        scratch_shapes=[
            pltpu.VMEM((width, 2 * width), jnp.float32),
            pltpu.VMEM((8, width), jnp.float32),
            pltpu.VMEM((packed_rows(width), LANES), jnp.float32),
        ],
        name="gram_rows",
    )(me, x)


def partner(x, axis, size, offset):
    return lax.ppermute(x, axis, [(i, i ^ offset) for i in range(size)])


def reduce_all(pieces, groups):
    n = len(pieces)
    arrived = [partner(pieces[d], "pencil", n, d) for d in range(1, n)]
    total = pieces[0]
    for piece in arrived:
        total = total + piece
    offset = 1
    while offset < groups:
        total = total + partner(total, "bulk", groups, offset)
        offset *= 2
    return [total] + [partner(total, "pencil", n, d) for d in range(1, n)]


def eliminate(w):
    n = w.shape[0]
    lane = lax.broadcasted_iota(jnp.int32, (8, n), 1)
    sub = lax.broadcasted_iota(jnp.int32, (8, n), 0)

    def full(x):
        return jnp.broadcast_to(x, (8, n))

    out = []
    for base in range(0, n, SUPER):
        count = SUPER // 8
        rows = [w[8 * v : 8 * v + 8] for v in range(count)]
        inverses = []
        for t in range(count):
            k = base + 8 * t
            inside = (lane >= k) & (lane < k + 8)
            cols = [[full(rows[v][:, k + j : k + j + 1]) for v in range(t, count)] for j in range(8)]
            rows[t] = jnp.where(inside, jnp.where(lane - k == sub, 1.0, 0.0), rows[t])
            for v in range(t + 1, count):
                rows[v] = jnp.where(inside, 0.0, rows[v])
            inverse = jnp.zeros((8, n), jnp.float32)
            for j in range(8):
                pivot = 1.0 / full(cols[j][0][j : j + 1])
                inverse = jnp.where(sub == j, pivot, inverse)
                below = [jnp.where(sub > j, cols[j][0], 0.0)] + cols[j][1:]
                factors = [x * pivot for x in below]
                for q in range(j + 1, 8):
                    head = full(cols[q][0][j : j + 1])
                    cols[q] = [x - factor * head for x, factor in zip(cols[q], factors)]
                head = full(rows[t][j : j + 1])
                for v in range(t, count):
                    rows[v] = rows[v] - factors[v - t] * head
            inverses.append(inverse)
            rows[t] = jnp.where((lane >= k + 8) & (lane < base + SUPER), 0.0, rows[t])
        panel, inverse = jnp.concatenate(rows, 0), jnp.concatenate(inverses, 0)
        lanes = lax.broadcasted_iota(jnp.int32, panel.shape, 1)
        out.append(jnp.where(lanes < base + SUPER, panel * jnp.sqrt(inverse), 0.0))
        left = n - base - SUPER
        if left:
            update = exact(panel * inverse, panel, 0, 0)[base + SUPER :]
            lanes = lax.broadcasted_iota(jnp.int32, (left, n), 1)
            w = jnp.where((lanes >= base) & (lanes < base + SUPER), 0.0, w[SUPER:]) - update
    return jnp.concatenate(out, 0)


def subspace_kernel(n, me_ref, *refs):
    pieces, (start_ref, out_ref, packed, gram, sems) = refs[:n], refs[n:]
    rows = pieces[0].shape[0]
    copies = []
    for d, piece in enumerate(pieces):
        at = pl.multiple_of((me_ref[0] ^ d) * rows, 8)
        copies.append(pltpu.make_async_copy(piece, packed.at[pl.ds(at, rows), :], sems.at[d]))
        copies[-1].start()
    out_ref[...] = start_ref[...]
    for copy in copies:
        copy.wait()
    for place, (p, q) in enumerate(upper_blocks(gram.shape[0])):
        block = packed[place * LANES : (place + 1) * LANES]
        gram[p * LANES : (p + 1) * LANES, q * LANES : (q + 1) * LANES] = block
        if p != q:
            gram[q * LANES : (q + 1) * LANES, p * LANES : (p + 1) * LANES] = block.T

    def iteration(_, carry):
        grown = exact(gram[...], out_ref[...], 1, 0)
        out_ref[...] = exact(grown, eliminate(exact(grown, grown, 0, 0)), 1, 1)
        return carry

    lax.fori_loop(0, ITERS, iteration, 0)


def subspace(me, pieces, start):
    width = start.shape[0]
    n = len(pieces)
    vmem = pl.BlockSpec(memory_space=pltpu.VMEM)
    return pl.pallas_call(
        functools.partial(subspace_kernel, n),
        in_specs=[SCALAR] + [pl.BlockSpec(memory_space=pl.ANY)] * n + [vmem],
        out_specs=vmem,
        out_shape=jax.ShapeDtypeStruct(start.shape, jnp.float32),
        scratch_shapes=[
            pltpu.VMEM((packed_rows(width), LANES), jnp.float32),
            pltpu.VMEM((width, width), jnp.float32),
            pltpu.SemaphoreType.DMA((n,)),
        ],
        name="subspace",
    )(me, *pieces, start)


def project_kernel(n, me_ref, x_ref, basis_ref, *refs):
    out_refs, (bases,) = refs[:-1], refs[-1:]
    groups, _, cols, width = x_ref.shape
    rank = basis_ref.shape[1]
    share = rank // n

    @pl.when(pl.program_id(0) == 0)
    def _():
        basis = basis_ref[...]
        for m in range(n):
            turned = pltpu.roll(basis, m * share, 1) if m else basis
            bases[m] = jnp.concatenate(split(turned), 1)

    projected = []
    for m in range(n):
        high, low = split(x_ref[:, m].reshape(groups * cols, width))
        sums = mul(high, bases[m], 1, 0)
        low_sums = mul(low, bases[m][:, :rank], 1, 0)
        projected.append(sums[:, :rank] + sums[:, rank:] + low_sums)
    slot = lax.broadcasted_iota(jnp.int32, (1, rank), 1) // share
    for d, out_ref in enumerate(out_refs):
        item = lax.rem(slot - (me_ref[0] ^ d) + n, n)
        for g in range(groups):
            piece = projected[0][g * cols : (g + 1) * cols]
            for m in range(1, n):
                piece = jnp.where(item == m, projected[m][g * cols : (g + 1) * cols], piece)
            out_ref[:, g * rank : (g + 1) * rank] = piece


def project(me, x, basis, first, steps):
    _, n, cols, width = x.shape
    rank = basis.shape[1]
    return pl.pallas_call(
        functools.partial(project_kernel, n),
        grid=(steps,),
        in_specs=[
            SCALAR,
            pl.BlockSpec((GROUPS, n, cols, width), lambda i: (first + i, 0, 0, 0)),
            pl.BlockSpec((width, rank), lambda i: (0, 0)),
        ],
        out_specs=[pl.BlockSpec((cols, GROUPS * rank), lambda i: (0, i))] * n,
        out_shape=[jax.ShapeDtypeStruct((cols, steps * GROUPS * rank), jnp.float32)] * n,
        scratch_shapes=[pltpu.VMEM((n, width, 2 * rank), jnp.bfloat16)],
        cost_estimate=pl.CostEstimate(
            flops=6 * steps * GROUPS * n * cols * width * rank,
            bytes_accessed=4 * steps * GROUPS * n * cols * (width + rank),
            transcendentals=0,
        ),
        name="project",
    )(me, x, basis)


def load_stacked(me_ref, pieces, both):
    cols = pieces[0].shape[0]
    width = both.shape[0] // 2
    for d, piece in enumerate(pieces):
        at = pl.multiple_of((me_ref[0] ^ d) * cols, 16)
        high, low = split(piece[...])
        both[pl.ds(at, cols), :] = high
        both[pl.ds(width + at, cols), :] = low


def chunk_index(starts, chunk, tile):
    return lambda i: (0, jnp.clip(i - starts[chunk], 0, starts[chunk + 1] - starts[chunk] - 1))


def over_chunks(me_ref, starts, pieces, n, both):
    for chunk in range(len(starts) - 1):

        @pl.when((pl.program_id(0) >= starts[chunk]) & (pl.program_id(0) < starts[chunk + 1]))
        def _():
            load_stacked(me_ref, pieces[chunk * n : (chunk + 1) * n], both)


def chunk_starts(pieces, tile):
    starts = [0]
    for group in pieces:
        starts.append(starts[-1] + group[0].shape[1] // tile)
    return starts


def gram_cols_kernel(starts, n, carried, final, me_ref, *refs):
    count = (len(starts) - 1) * n
    pieces, refs = refs[:count], refs[count:]
    before, refs = (refs[:1], refs[1:]) if carried else (None, refs)
    if final:
        out_refs, (sums, both, packed) = refs[:n], refs[n:]
    else:
        sums, both = refs
    width = both.shape[0] // 2

    @pl.when(pl.program_id(0) == 0)
    def _():
        sums[...] = before[0][...] if carried else jnp.zeros_like(sums)

    over_chunks(me_ref, starts, pieces, n, both)
    sums[...] += mul(both[:width], both[...], 1, 1)
    sums[:, :width] += mul(both[width:], both[width:], 1, 1)

    if final:

        @pl.when(pl.program_id(0) == pl.num_programs(0) - 1)
        def _():
            cross = sums[:, width:]
            store_pieces(me_ref, sums[:, :width] + cross + cross.T, packed, out_refs)


def gram_cols(me, pieces, tile, before, final):
    n = len(pieces[0])
    cols = pieces[0][0].shape[0]
    width = n * cols
    starts = chunk_starts(pieces, tile)
    shape = (width, 2 * width)
    whole = pl.BlockSpec(shape, lambda i: (0, 0))
    sums, both = pltpu.VMEM(shape, jnp.float32), pltpu.VMEM((2 * width, tile), jnp.bfloat16)
    if final:
        out_specs, out_shape = piece_outputs(n, width)
        scratch = [sums, both, pltpu.VMEM((packed_rows(width), LANES), jnp.float32)]
    else:
        out_specs, out_shape = whole, jax.ShapeDtypeStruct(shape, jnp.float32)
        scratch = [both]
    return pl.pallas_call(
        functools.partial(gram_cols_kernel, starts, n, before is not None, final),
        grid=(starts[-1],),
        in_specs=[SCALAR]
        + [
            pl.BlockSpec((cols, tile), chunk_index(starts, chunk, tile))
            for chunk in range(len(pieces))
            for _ in range(n)
        ]
        + [whole] * (before is not None),
        out_specs=out_specs,
        out_shape=out_shape,
        scratch_shapes=scratch,
        cost_estimate=pl.CostEstimate(
            flops=6 * width * width * tile * starts[-1],
            bytes_accessed=4 * width * tile * starts[-1],
            transcendentals=0,
        ),
        name="gram_cols",
    )(me, *[x for group in pieces for x in group], *([] if before is None else [before]))


def core_kernel(starts, n, me_ref, *refs):
    count = (len(starts) - 1) * n
    pieces, (basis_ref, out_ref, basis, both) = refs[:count], refs[count:]
    width, rank = basis_ref.shape
    share = rank // n

    @pl.when(pl.program_id(0) == 0)
    def _():
        basis[...] = jnp.concatenate(split(basis_ref[...].T), 0)

    over_chunks(me_ref, starts, pieces, n, both)
    sums = mul(basis[...], both[:width], 1, 0)
    result = sums[:rank] + sums[rank:] + mul(basis[:rank], both[width:], 1, 0)
    for g in range(result.shape[1] // rank):
        turned = result[:, g * rank : (g + 1) * rank].T
        for s in range(n):
            item = lax.rem(s - me_ref[0] + n, n)
            at = pl.multiple_of(g * rank + item * share, 8)
            out_ref[pl.ds(at, share), :] = turned[s * share : (s + 1) * share]


def core(me, pieces, tile, basis):
    n = len(pieces[0])
    cols = pieces[0][0].shape[0]
    width, rank = basis.shape
    starts = chunk_starts(pieces, tile)
    return pl.pallas_call(
        functools.partial(core_kernel, starts, n),
        grid=(starts[-1],),
        in_specs=[SCALAR]
        + [
            pl.BlockSpec((cols, tile), chunk_index(starts, chunk, tile))
            for chunk in range(len(pieces))
            for _ in range(n)
        ]
        + [pl.BlockSpec(basis.shape, lambda i: (0, 0))],
        out_specs=pl.BlockSpec((tile, rank), lambda i: (i, 0)),
        out_shape=jax.ShapeDtypeStruct((starts[-1] * tile, rank), jnp.float32),
        scratch_shapes=[
            pltpu.VMEM((2 * rank, width), jnp.bfloat16),
            pltpu.VMEM((2 * width, tile), jnp.bfloat16),
        ],
        name="core",
    )(me, *[x for group in pieces for x in group], basis)


def chunk_steps(total):
    if total < 4:
        return [1] * total
    middle = total - 2
    return [1] + [2] * (middle // 2) + [1] * (middle % 2) + [1]


def per_device(n, groups, density, start_first, start_second):
    snap_count, cell_count, my_cols, mode_width = density.shape
    rank = start_first.shape[1]
    place = lax.axis_index("pencil")
    me = place.astype(jnp.int32).reshape(1)
    items = density.reshape(snap_count * cell_count // n, n, my_cols, mode_width)
    tile = GROUPS * rank

    pieces = gram_rows(me, density.reshape(-1, mode_width), n)
    factor_first = subspace(me, reduce_all(pieces, groups), start_first)

    exchanged, first = [], 0
    for steps in chunk_steps(items.shape[0] // GROUPS):
        own, *sent = project(me, items, factor_first, first, steps)
        exchanged.append([own] + [partner(x, "pencil", n, d + 1) for d, x in enumerate(sent)])
        first += steps

    sums = gram_cols(me, exchanged[:-1], tile, None, False)
    pieces = gram_cols(me, exchanged[-1:], tile, sums, True)
    factor_second = subspace(me, reduce_all(pieces, groups), start_second)

    core_tensor = core(me, exchanged, tile, factor_second)
    core_tensor = core_tensor.reshape(snap_count, cell_count, rank // n, factor_second.shape[1])
    return (core_tensor, factor_first, factor_second)


def solution(mesh):
    placed = (P(None, "bulk", "pencil", None), P(), P())
    return jax.shard_map(
        functools.partial(per_device, mesh.shape["pencil"], mesh.shape["bulk"]),
        mesh=mesh,
        in_specs=placed,
        out_specs=(P(None, "bulk", "pencil", None), P(), P()),
        check_vma=False,
    )
```
